32 devices in a mesh: sub: 8 (over z, x), blk: 4 (over y, core).
Axes of the slice: x: 2, y: 2, z: 4, core: 2. Of those that a mesh axis runs over, the one named last changes fastest.
Arguments:
- coefficients: float32 [512, 4, 2, 64, 128], P('sub', None, None, 'blk'), may hold values from -0.2 to 0.2
- owner_slot: int32 [512], P('sub'), may hold values from 0 to 511, as said below
- child_list: int32 [512, 8], P('sub'), may hold values from 0 to 7, each once within a row
Outputs:
- children: float32 [512, 4, 8, 64, 2, 128], P('sub', None, None, 'blk')
The draws below stay inside these ranges and needn't reach their ends.
Inputs may be any that keep to these rules, and one draw needn't show every extreme that they name: owner_slot is a permutation of the 512 positions; position s belongs to subtree index s // 64; of the 64 boxes held by one subtree index exactly 8 belong to each subtree index. `child_list`: each row lists the 8 octant codes once each.
All inputs are finite; a program needn't handle non-finite values.
Results may differ from the reference program's by a relative error of at most 0.0003.
Values sent between devices are 32-bit elements; how exact they have to be, the bound alone decides.
A program may use at most 128 MiB of HBM per device.

```python
import jax
import jax.numpy as jnp
from jax import lax

L = 64
M = 128
J = 64
K = 128
BOX_DEV = 64
NRHS = 4
BOXES = 512


def draw_owner_slot(key, part):
    sub_count = BOXES // BOX_DEV
    per_peer = BOX_DEV // sub_count
    first_key, second_key = jax.random.split(jax.random.fold_in(key, 11), 2)
    local_order = jax.vmap(lambda one: jax.random.permutation(one, BOX_DEV))(jax.random.split(first_key, sub_count))
    inside = jax.vmap(lambda one: jax.random.permutation(one, BOX_DEV))(jax.random.split(second_key, sub_count))
    ranks = jnp.arange(BOX_DEV, dtype=jnp.int32)
    target = ranks // per_peer
    within = ranks % per_peer
    sources = jnp.arange(sub_count, dtype=jnp.int32)[:, None]
    positions = inside[target[None, :], sources * per_peer + within[None, :]]
    slot_by_rank = target[None, :] * BOX_DEV + positions
    inverse = jnp.argsort(local_order, axis=1)
    slots = jnp.take_along_axis(slot_by_rank, inverse, axis=1)
    return slots.reshape(BOXES).astype(jnp.int32)


def steps_of(own_key, shape, cuts, least, largest):
    loudness, own = 1.0, jax.random.fold_in(own_key, 6)
    for position, blocks in cuts:
        heights = jnp.exp(jax.random.uniform(jax.random.fold_in(own, position), (blocks,), jnp.float32, least / len(cuts), largest / len(cuts)))
        loudness = loudness * jnp.repeat(heights, shape[position] // blocks).reshape([-1 if axis == position else 1 for axis in range(len(shape))])
    return loudness


def centred(rng, extent, width, reach, cuts=(), kind=jnp.bfloat16):
    entries = width * jax.random.normal(rng, extent, jnp.float32)
    if cuts:
        entries = entries * steps_of(rng, extent, cuts, -0.22, 0.18)
    return jnp.clip(entries, -reach, reach).astype(kind)


def setup_inputs(seed: int = 0) -> dict:
    key_of = jax.random.split(jax.random.key(seed), 4)
    coefficients = centred(key_of[0], (BOXES, NRHS, 2, L, M), 0.03, 0.2, ((0, 8), (3, 4)), jnp.float32)
    owner_slot = draw_owner_slot(jax.random.fold_in(key_of[3], 71), 0)
    child_list = jax.vmap(lambda own: jax.random.permutation(own, 8))(jax.random.split(key_of[2], BOXES)).reshape((BOXES, 8)).astype(jnp.int32)
    return {"coefficients": coefficients, "owner_slot": owner_slot, "child_list": child_list}


def legendre_table(orders_abs, polar, degrees):
    cosines = jnp.cos(polar)[None, :]
    sines = jnp.sin(polar)[None, :]
    order_col = orders_abs[:, None]
    log_start = 0.5 * (jnp.log((2.0 * order_col + 1.0) / (4.0 * jnp.pi)) + lax.lgamma(2.0 * order_col + 1.0) - order_col * jnp.log(4.0) - 2.0 * lax.lgamma(order_col + 1.0)) + order_col * jnp.log(sines)
    diag_value = jnp.exp(log_start)
    next_value = jnp.sqrt(2.0 * order_col + 3.0) * cosines * diag_value

    def advance(state, degree):
        previous, before, factor_prev = state
        numer = jnp.maximum(4.0 * degree * degree - 1.0, 1.0)
        denom = jnp.maximum(degree * degree - order_col * order_col, 1.0)
        factor = jnp.sqrt(numer / denom)
        recur = factor * (cosines * previous - before / factor_prev)
        value = jnp.where(degree < order_col, 0.0, jnp.where(degree == order_col, diag_value, jnp.where(degree == order_col + 1.0, next_value, recur)))
        return ((value, previous, factor), value)
    zeros = jnp.zeros_like(diag_value)
    start_state = (zeros, zeros, jnp.ones_like(order_col))
    _, values = lax.scan(advance, start_state, jnp.arange(degrees).astype(jnp.float32))
    return values

def dft_table(degrees, columns, azimuths):
    column_ids = jnp.arange(columns, dtype=jnp.int32)
    azimuth_ids = jnp.arange(azimuths, dtype=jnp.int32)
    turns = jnp.mod((column_ids[:, None] - degrees) * azimuth_ids[None, :], azimuths)
    angle = 2.0 * jnp.pi * turns.astype(jnp.float32) / azimuths
    cosine = jnp.cos(angle)
    sine = jnp.sin(angle)
    upper = jnp.concatenate([cosine, sine], axis=1)
    lower = jnp.concatenate([-sine, cosine], axis=1)
    return jnp.concatenate([upper, lower], axis=0)

def shift_children(waves, octants, polar, azimuths):
    azimuth = 2.0 * jnp.pi * jnp.arange(azimuths).astype(jnp.float32) / azimuths
    dir_x = jnp.sin(polar)[:, None] * jnp.cos(azimuth)[None, :]
    dir_y = jnp.sin(polar)[:, None] * jnp.sin(azimuth)[None, :]
    dir_z = jnp.cos(polar)[:, None] * jnp.ones_like(azimuth)[None, :]
    sign_x = (2 * (octants & 1) - 1).astype(jnp.float32)[:, None, None]
    sign_y = (2 * (octants >> 1 & 1) - 1).astype(jnp.float32)[:, None, None]
    sign_z = (2 * (octants >> 2 & 1) - 1).astype(jnp.float32)[:, None, None]
    phase = 5.5 * (sign_x * dir_x[None] + sign_y * dir_y[None] + sign_z * dir_z[None])
    phase_cos = jnp.cos(phase)[None]
    phase_sin = jnp.sin(phase)[None]
    wave_re = waves[:, :, 0, :][:, None]
    wave_im = waves[:, :, 1, :][:, None]
    real_part = wave_re * phase_cos - wave_im * phase_sin
    imag_part = wave_re * phase_sin + wave_im * phase_cos
    return jnp.stack([real_part, imag_part], axis=-2)

def reference(coefficients, owner_slot, child_list):
    owned = coefficients[jnp.argsort(owner_slot)]
    polar = jnp.pi * (jnp.arange(J).astype(jnp.float32) + 0.5) / J
    orders_abs = jnp.abs(jnp.arange(M) - L).astype(jnp.float32)
    table = legendre_table(orders_abs, polar, L)
    spectral = dft_table(L, M, K)
    cases = coefficients.shape[1]

    def one_box(inputs):
        expansion, octants = inputs
        cycles = jnp.einsum('rxlc,lcj->rjxc', expansion, table, precision=lax.Precision.HIGHEST)
        waves = jnp.dot(cycles.reshape(cases * J, 2 * M), spectral, precision=lax.Precision.HIGHEST)
        return shift_children(waves.reshape(cases, J, 2, K), octants, polar, K)
    return lax.map(one_box, (owned, child_list))
```

```python
import functools
import math

import jax
import jax.numpy as jnp
import numpy as np
from jax import lax
from jax.experimental import pallas as pl
from jax.experimental.pallas import tpu as pltpu
from jax.sharding import PartitionSpec as P

J = 64
K = 128
GROUP = 4


def legendre_constants(degrees, columns):
    q = np.abs(np.arange(columns) - degrees).astype(np.float64)
    log_norm = np.array(
        [
            0.5
            * (
                math.log((2 * v + 1) / (4 * math.pi))
                + math.lgamma(2 * v + 1)
                - v * math.log(4.0)
                - 2 * math.lgamma(v + 1)
            )
            for v in q
        ]
    )
    l = np.arange(degrees, dtype=np.float64)[:, None]
    numer = np.maximum(4 * l * l - 1, 1.0)
    denom = np.maximum(l * l - q[None] ** 2, 1.0)
    factor = np.sqrt(numer / denom)
    before = np.ones_like(factor)
    before[1:] = 1.0 / factor[:-1]
    return (
        log_norm.astype(np.float32)[None],
        q.astype(np.float32)[None],
        factor.astype(np.float32)[:, None, :],
        before.astype(np.float32)[:, None, :],
    )


def wave_matrix(degrees, columns, azimuths):
    turns = ((np.arange(columns)[:, None] - degrees) * np.arange(azimuths)[None, :]) % azimuths
    angle = 2.0 * np.pi * turns / azimuths
    cosine, sine = np.cos(angle), np.sin(angle)
    left = np.concatenate([cosine, -sine], axis=0)
    right = np.concatenate([-sine, -cosine], axis=0)
    return np.concatenate([left, right], axis=1).astype(np.float32)


def phase_tables(polar, azimuths):
    azimuth = 2.0 * jnp.pi * jnp.arange(azimuths).astype(jnp.float32) / azimuths
    octants = jnp.arange(8, dtype=jnp.int32)
    dir_x = jnp.sin(polar)[:, None] * jnp.cos(azimuth)[None, :]
    dir_y = jnp.sin(polar)[:, None] * jnp.sin(azimuth)[None, :]
    dir_z = jnp.cos(polar)[:, None] * jnp.ones_like(azimuth)[None, :]
    sign_x = (2 * (octants & 1) - 1).astype(jnp.float32)[:, None, None]
    sign_y = (2 * (octants >> 1 & 1) - 1).astype(jnp.float32)[:, None, None]
    sign_z = (2 * (octants >> 2 & 1) - 1).astype(jnp.float32)[:, None, None]
    phase = 5.5 * (sign_x * dir_x[None] + sign_y * dir_y[None] + sign_z * dir_z[None])
    return jnp.repeat(jnp.cos(phase), 2, axis=1), jnp.repeat(jnp.sin(phase), 2, axis=1)


def fill_table(tab, diag_ref, cos_ref, order_ref, factor_ref, before_ref):
    degrees = tab.shape[0]
    diag = diag_ref[...]
    cosines = cos_ref[...]
    order = jnp.broadcast_to(order_ref[...], diag.shape)
    next_value = jnp.sqrt(2.0 * order + 3.0) * cosines * diag

    def advance(degree, state):
        previous, before = state
        level = lax.convert_element_type(degree, jnp.float32)
        recur = factor_ref[degree] * (cosines * previous - before * before_ref[degree])
        value = jnp.where(level == order + 1.0, next_value, recur)
        value = jnp.where(level == order, diag, value)
        value = jnp.where(level < order, 0.0, value)
        tab[degree] = value
        return value, previous

    zeros = diag - diag
    lax.fori_loop(0, degrees, advance, (zeros, zeros))


def transform(source, child, *refs):
    coefs = refs[:GROUP]
    diag, cosines, order, factor, before, matrix, phase_cos, phase_sin, out, tab, upper, lower = refs[GROUP:]
    step = pl.program_id(0)

    @pl.when(step == 0)
    def _():
        fill_table(tab, diag, cosines, order, factor, before)

    parts, _, cases, _, depth, columns = coefs[0].shape
    width = tab.shape[1]
    rows = 2 * width
    for box in range(GROUP):
        coef = coefs[box]

        def add(part, totals):
            totals = list(totals)
            for inner in range(depth):
                weight = tab[part * depth + inner]
                for case in range(cases):
                    for half in range(2):
                        value = coef[part, 0, case, half, pl.ds(inner, 1), :]
                        slot = case * 2 + half
                        totals[slot] = totals[slot] + jnp.broadcast_to(value, (width, columns)) * weight
            return tuple(totals)

        zeros = tab[0] - tab[0]
        totals = lax.fori_loop(0, parts, add, (zeros,) * (2 * cases))
        for case in range(cases):
            base = (box * cases + case) * rows
            real, imag = totals[2 * case], totals[2 * case + 1]
            upper[pl.ds(base, width, 2), :] = real
            upper[pl.ds(base + 1, width, 2), :] = imag
            lower[pl.ds(base, width, 2), :] = imag
            lower[pl.ds(base + 1, width, 2), :] = -real
    both = jnp.concatenate([upper[...], lower[...]], axis=1)
    spread = jnp.dot(both, matrix[...], precision=lax.Precision.HIGHEST, preferred_element_type=jnp.float32)
    for box in range(GROUP):
        for place in range(8):
            octant = child[(step * GROUP + box) * 8 + place]
            turn_cos = phase_cos[octant]
            turn_sin = phase_sin[octant]
            for case in range(cases):
                base = (box * cases + case) * rows
                wave = spread[base : base + rows, :K]
                quarter = spread[base : base + rows, K:]
                out[box, case, place] = wave * turn_cos + quarter * turn_sin


def make_children(gathered, source, child_list, blk_index):
    parts, boxes, cases, _, depth, columns = gathered.shape
    degrees = parts * depth
    width = J // parts
    polar_all = jnp.pi * (jnp.arange(J).astype(jnp.float32) + 0.5) / J
    polar = lax.dynamic_slice_in_dim(polar_all, blk_index * width, width, 0)
    log_norm, order, factor, before = legendre_constants(degrees, columns)
    diag = jnp.exp(log_norm + order * jnp.log(jnp.sin(polar))[:, None])
    cosines = jnp.broadcast_to(jnp.cos(polar)[:, None], (width, columns))
    phase_cos, phase_sin = phase_tables(polar, K)
    matrix = jnp.asarray(wave_matrix(degrees, columns, K))

    def pick(offset):
        return pl.BlockSpec(
            (parts, 1, cases, 2, depth, columns),
            lambda i, source, child: (0, source[i * GROUP + offset], 0, 0, 0, 0),
        )

    whole = pl.BlockSpec(memory_space=pltpu.VMEM)
    rows = GROUP * cases * 2 * width
    out = pl.pallas_call(
        transform,
        grid_spec=pltpu.PrefetchScalarGridSpec(
            num_scalar_prefetch=2,
            grid=(boxes // GROUP,),
            in_specs=[pick(n) for n in range(GROUP)] + [whole] * 8,
            out_specs=pl.BlockSpec(
                (GROUP, cases, 8, 2 * width, K), lambda i, source, child: (i, 0, 0, 0, 0)
            ),
            scratch_shapes=[
                pltpu.VMEM((degrees, width, columns), jnp.float32),
                pltpu.VMEM((rows, columns), jnp.float32),
                pltpu.VMEM((rows, columns), jnp.float32),
            ],
        ),
        out_shape=jax.ShapeDtypeStruct((boxes, cases, 8, 2 * width, K), jnp.float32),
        compiler_params=pltpu.CompilerParams(vmem_limit_bytes=40 * 1024 * 1024),
        name="transform",
    )(
        source,
        child_list.reshape(-1),
        *([gathered] * GROUP),
        diag,
        cosines,
        jnp.asarray(order),
        jnp.asarray(factor),
        jnp.asarray(before),
        matrix,
        phase_cos,
        phase_sin,
    )
    return out.reshape(boxes, cases, 8, width, 2, K)


def body(coefficients, owner_slot, child_list):
    box_count = coefficients.shape[0]
    sub_count = lax.axis_size("sub")
    per_peer = box_count // sub_count
    targets = owner_slot // box_count
    positions = owner_slot % box_count
    send_order = jnp.argsort(targets, stable=True)
    outgoing = coefficients[send_order].reshape((sub_count, per_peer) + coefficients.shape[1:])
    placed = positions[send_order].reshape(sub_count, per_peer)
    arrived = lax.all_to_all(outgoing, "sub", split_axis=0, concat_axis=0, tiled=True)
    arrived_slots = lax.all_to_all(placed, "sub", split_axis=0, concat_axis=0, tiled=True)
    source = jnp.argsort(arrived_slots.reshape(-1)).astype(jnp.int32)
    gathered = lax.all_gather(arrived.reshape(coefficients.shape), "blk")
    return make_children(gathered, source, child_list, lax.axis_index("blk"))


def solution(mesh):
    placed = (P("sub", None, None, "blk", None), P("sub"), P("sub", None))
    return jax.shard_map(
        body,
        mesh=mesh,
        in_specs=placed,
        out_specs=P("sub", None, None, "blk", None, None),
        check_vma=False,
    )
```

```python
import functools
import math

import jax
import jax.numpy as jnp
import numpy as np
from jax import lax
from jax.experimental import pallas as pl
from jax.experimental.pallas import tpu as pltpu
from jax.sharding import PartitionSpec as P

J = 64
K = 128
GROUP = 4


def legendre_constants(degrees, columns):
    q = np.abs(np.arange(columns) - degrees).astype(np.float64)
    log_norm = np.array(
        [
            0.5
            * (
                math.log((2 * v + 1) / (4 * math.pi))
                + math.lgamma(2 * v + 1)
                - v * math.log(4.0)
                - 2 * math.lgamma(v + 1)
            )
            for v in q
        ]
    )
    l = np.arange(degrees, dtype=np.float64)[:, None]
    numer = np.maximum(4 * l * l - 1, 1.0)
    denom = np.maximum(l * l - q[None] ** 2, 1.0)
    factor = np.sqrt(numer / denom)
    before = np.ones_like(factor)
    before[1:] = 1.0 / factor[:-1]
    return (
        log_norm.astype(np.float32)[None],
        q.astype(np.float32)[None],
        factor.astype(np.float32)[:, None, :],
        before.astype(np.float32)[:, None, :],
    )


def wave_matrix(degrees, columns, azimuths):
    turns = ((np.arange(columns)[:, None] - degrees) * np.arange(azimuths)[None, :]) % azimuths
    angle = 2.0 * np.pi * turns / azimuths
    cosine, sine = np.cos(angle), np.sin(angle)
    left = np.concatenate([cosine, -sine], axis=0)
    right = np.concatenate([-sine, -cosine], axis=0)
    return np.concatenate([left, right], axis=1).astype(np.float32)


def phase_tables(polar, azimuths):
    azimuth = 2.0 * jnp.pi * jnp.arange(azimuths).astype(jnp.float32) / azimuths
    octants = jnp.arange(8, dtype=jnp.int32)
    dir_x = jnp.sin(polar)[:, None] * jnp.cos(azimuth)[None, :]
    dir_y = jnp.sin(polar)[:, None] * jnp.sin(azimuth)[None, :]
    dir_z = jnp.cos(polar)[:, None] * jnp.ones_like(azimuth)[None, :]
    sign_x = (2 * (octants & 1) - 1).astype(jnp.float32)[:, None, None]
    sign_y = (2 * (octants >> 1 & 1) - 1).astype(jnp.float32)[:, None, None]
    sign_z = (2 * (octants >> 2 & 1) - 1).astype(jnp.float32)[:, None, None]
    phase = 5.5 * (sign_x * dir_x[None] + sign_y * dir_y[None] + sign_z * dir_z[None])
    return jnp.repeat(jnp.cos(phase), 2, axis=1), jnp.repeat(jnp.sin(phase), 2, axis=1)


def fill_table(tab, diag_ref, cos_ref, order_ref, factor_ref, before_ref):
    degrees = tab.shape[0]
    diag = diag_ref[...]
    cosines = cos_ref[...]
    order = jnp.broadcast_to(order_ref[...], diag.shape)
    next_value = jnp.sqrt(2.0 * order + 3.0) * cosines * diag

    def advance(degree, state):
        previous, before = state
        level = lax.convert_element_type(degree, jnp.float32)
        recur = factor_ref[degree] * (cosines * previous - before * before_ref[degree])
        value = jnp.where(level == order + 1.0, next_value, recur)
        value = jnp.where(level == order, diag, value)
        value = jnp.where(level < order, 0.0, value)
        tab[degree] = value
        return value, previous

    zeros = diag - diag
    lax.fori_loop(0, degrees, advance, (zeros, zeros))


def transform(source, child, *refs):
    coefs = refs[:GROUP]
    diag, cosines, order, factor, before, matrix, phase_cos, phase_sin, out, tab, upper, lower = refs[GROUP:]
    step = pl.program_id(0)

    @pl.when(step == 0)
    def _():
        fill_table(tab, diag, cosines, order, factor, before)

    parts, _, cases, _, depth, columns = coefs[0].shape
    width = tab.shape[1]
    rows = 2 * width
    for box in range(GROUP):
        coef = coefs[box]

        def add(part, totals):
            totals = list(totals)
            for inner in range(depth):
                weight = tab[part * depth + inner]
                for case in range(cases):
                    for half in range(2):
                        value = coef[part, 0, case, half, pl.ds(inner, 1), :]
                        slot = case * 2 + half
                        totals[slot] = totals[slot] + jnp.broadcast_to(value, (width, columns)) * weight
            return tuple(totals)

        zeros = tab[0] - tab[0]
        totals = lax.fori_loop(0, parts, add, (zeros,) * (2 * cases))
        for case in range(cases):
            base = (box * cases + case) * rows
            real, imag = totals[2 * case], totals[2 * case + 1]
            upper[pl.ds(base, width, 2), :] = real
            upper[pl.ds(base + 1, width, 2), :] = imag
            lower[pl.ds(base, width, 2), :] = imag
            lower[pl.ds(base + 1, width, 2), :] = -real
    both = jnp.concatenate([upper[...], lower[...]], axis=1)
    spread = jnp.dot(both, matrix[...], precision=lax.Precision.HIGHEST, preferred_element_type=jnp.float32)
    for box in range(GROUP):
        for place in range(8):
            octant = child[(step * GROUP + box) * 8 + place]
            turn_cos = phase_cos[octant]
            turn_sin = phase_sin[octant]
            for case in range(cases):
                base = (box * cases + case) * rows
                wave = spread[base : base + rows, :K]
                quarter = spread[base : base + rows, K:]
                out[box, case, place] = wave * turn_cos + quarter * turn_sin


def make_children(gathered, source, child_list, blk_index):
    parts, boxes, cases, _, depth, columns = gathered.shape
    degrees = parts * depth
    width = J // parts
    polar_all = jnp.pi * (jnp.arange(J).astype(jnp.float32) + 0.5) / J
    polar = lax.dynamic_slice_in_dim(polar_all, blk_index * width, width, 0)
    log_norm, order, factor, before = legendre_constants(degrees, columns)
    diag = jnp.exp(log_norm + order * jnp.log(jnp.sin(polar))[:, None])
    cosines = jnp.broadcast_to(jnp.cos(polar)[:, None], (width, columns))
    phase_cos, phase_sin = phase_tables(polar, K)
    matrix = jnp.asarray(wave_matrix(degrees, columns, K))

    def pick(offset):
        return pl.BlockSpec(
            (parts, 1, cases, 2, depth, columns),
            lambda i, source, child: (0, source[i * GROUP + offset], 0, 0, 0, 0),
        )

    whole = pl.BlockSpec(memory_space=pltpu.VMEM)
    rows = GROUP * cases * 2 * width
    out = pl.pallas_call(
        transform,
        grid_spec=pltpu.PrefetchScalarGridSpec(
            num_scalar_prefetch=2,
            grid=(boxes // GROUP,),
            in_specs=[pick(n) for n in range(GROUP)] + [whole] * 8,
            out_specs=pl.BlockSpec(
                (GROUP, cases, 8, 2 * width, K), lambda i, source, child: (i, 0, 0, 0, 0)
            ),
            scratch_shapes=[
                pltpu.VMEM((degrees, width, columns), jnp.float32),
                pltpu.VMEM((rows, columns), jnp.float32),
                pltpu.VMEM((rows, columns), jnp.float32),
            ],
        ),
        out_shape=jax.ShapeDtypeStruct((boxes, cases, 8, 2 * width, K), jnp.float32),
        compiler_params=pltpu.CompilerParams(vmem_limit_bytes=40 * 1024 * 1024),
        name="transform",
    )(
        source,
        child_list.reshape(-1),
        *([gathered] * GROUP),
        diag,
        cosines,
        jnp.asarray(order),
        jnp.asarray(factor),
        jnp.asarray(before),
        matrix,
        phase_cos,
        phase_sin,
    )
    return out.reshape(boxes, cases, 8, width, 2, K)


def swapped(index, step, size):
    total = 0
    bit = 1
    while bit < size:
        total = total + ((index // bit + step // bit) % 2) * bit
        bit *= 2
    return total


def exchange(
    sub_count,
    chips,
    blocks,
    slots,
    gathered,
    placed,
    send_far,
    recv_far,
    send_near,
    recv_near,
    send_pair,
    recv_pair,
    send_slot,
    recv_slot,
    local,
):
    per_peer = blocks.shape[1]
    steps = sub_count * per_peer
    sub = lax.axis_index("sub")
    blk = lax.axis_index("blk")
    chip = blk // 2
    core = blk % 2
    sibling = chip * 2 + (1 - core)

    def remote(source, target, send, recv, device):
        return pltpu.make_async_remote_copy(
            src_ref=source,
            dst_ref=target,
            send_sem=send,
            recv_sem=recv,
            device_id=device,
            device_id_type=pl.DeviceIdType.MESH,
        )

    def far(step, box):
        peer = swapped(sub, step, sub_count)
        return remote(
            blocks.at[peer, box],
            gathered.at[blk, sub, box],
            send_far.at[step, box],
            recv_far.at[step, box],
            (peer, blk),
        )

    def slot_copy(step):
        peer = swapped(sub, step, sub_count)
        return remote(slots.at[peer], placed.at[sub], send_slot.at[step], recv_slot.at[step], (peer, blk))

    def held(hop):
        return ((chip + chips - hop) % chips) * 2 + core

    def near(hop, step, box, own):
        source = swapped(sub, step, sub_count)
        origin = blocks.at[sub, box] if own else gathered.at[blk, source, box]
        return remote(
            origin,
            gathered.at[blk, source, box],
            send_near.at[hop - 1, step, box],
            recv_near.at[hop - 1, step, box],
            (sub, ((chip + hop) % chips) * 2 + core),
        )

    def pair(hop, step, box, own=False):
        source = swapped(sub, step, sub_count)
        part = held(hop)
        origin = blocks.at[sub, box] if own else gathered.at[part, source, box]
        return remote(
            origin,
            gathered.at[part, source, box],
            send_pair.at[hop, step, box],
            recv_pair.at[hop, step, box],
            (sub, sibling),
        )

    barrier = pltpu.get_barrier_semaphore()

    def greet(device):
        pl.semaphore_signal(barrier, inc=1, device_id=device, device_id_type=pl.DeviceIdType.MESH)

    for step in range(1, sub_count):
        greet((swapped(sub, step, sub_count), blk))
    for hop in range(1, chips):
        greet((sub, ((chip + hop) % chips) * 2 + core))
    greet((sub, sibling))
    pl.semaphore_wait(barrier, sub_count - 1 + chips)

    order = [step for step in range(sub_count // 2, sub_count)] + list(range(1, sub_count // 2))
    for step in order:
        slot_copy(step).start()

    @pl.loop(0, per_peer)
    def _(box):
        for step in order:
            far(step, box).start()

    keep_slot = pltpu.make_async_copy(slots.at[sub], placed.at[sub], local.at[0])
    keep_slot.start()
    keep_blocks = pltpu.make_async_copy(blocks.at[sub], gathered.at[blk, sub], local.at[1])
    keep_blocks.start()

    def relay(step, box):
        for hop in range(1, chips):
            near(hop, step, box, False).wait_recv()
            pair(hop, step, box).start()

    def arrive(step, box):
        if step > 0:
            far(step, box).wait_recv()
        for hop in range(1, chips):
            near(hop, step, box, step == 0).start()
        pair(0, step, box, step == 0).start()

    for step in range(sub_count):
        arrive(step, 0)

    @pl.loop(1, per_peer)
    def _(box):
        for step in range(sub_count):
            arrive(step, box)
            relay(step, box - 1)

    for step in range(sub_count):
        relay(step, per_peer - 1)

    @pl.loop(0, per_peer)
    def _(box):
        for step in range(sub_count):
            if step > 0:
                far(step, box).wait_send()
            for hop in range(1, chips):
                near(hop, step, box, step == 0).wait_send()
            for hop in range(chips):
                pair(hop, step, box, step == 0 and hop == 0).wait()

    for step in order:
        slot_copy(step).wait()
    keep_slot.wait()
    keep_blocks.wait()


def exchange_all(outgoing, slots, parts):
    sub_count, per_peer, rows, columns = outgoing.shape
    chips = parts // 2
    dma = pltpu.SemaphoreType.DMA
    anywhere = pl.BlockSpec(memory_space=pl.ANY)
    vmem = pl.BlockSpec(memory_space=pltpu.VMEM)
    hops = max(chips - 1, 1)
    return pl.pallas_call(
        functools.partial(exchange, sub_count, chips),
        out_shape=(
            jax.ShapeDtypeStruct((parts, sub_count, per_peer, rows, columns), jnp.float32),
            jax.ShapeDtypeStruct(slots.shape, jnp.int32),
        ),
        in_specs=[anywhere, vmem],
        out_specs=(anywhere, vmem),
        scratch_shapes=[
            dma((sub_count, per_peer)),
            dma((sub_count, per_peer)),
            dma((hops, sub_count, per_peer)),
            dma((hops, sub_count, per_peer)),
            dma((chips, sub_count, per_peer)),
            dma((chips, sub_count, per_peer)),
            dma((sub_count,)),
            dma((sub_count,)),
            dma((2,)),
        ],
        compiler_params=pltpu.CompilerParams(collective_id=0, has_side_effects=True),
        name="exchange",
    )(outgoing, slots)


def body(coefficients, owner_slot, child_list):
    box_count, cases, _, depth, columns = coefficients.shape
    sub_count = lax.axis_size("sub")
    parts = lax.axis_size("blk")
    per_peer = box_count // sub_count
    targets = owner_slot // box_count
    positions = owner_slot % box_count
    send_order = jnp.argsort(targets, stable=True)
    flat = coefficients.reshape(box_count, cases * 2 * depth, columns)
    outgoing = flat[send_order].reshape(sub_count, per_peer, cases * 2 * depth, columns)
    slots = positions[send_order].reshape(sub_count, 1, per_peer)
    slots = jnp.pad(slots, ((0, 0), (0, 0), (0, 128 - per_peer)))
    gathered, placed = exchange_all(outgoing, slots, parts)
    source = jnp.argsort(placed[:, 0, :per_peer].reshape(-1)).astype(jnp.int32)
    gathered = gathered.reshape(parts, box_count, cases, 2, depth, columns)
    return make_children(gathered, source, child_list, lax.axis_index("blk"))


def solution(mesh):
    placed = (P("sub", None, None, "blk", None), P("sub"), P("sub", None))
    return jax.shard_map(
        body,
        mesh=mesh,
        in_specs=placed,
        out_specs=P("sub", None, None, "blk", None, None),
        check_vma=False,
    )
```

```python
import functools
import math

import jax
import jax.numpy as jnp
import numpy as np
from jax import lax
from jax.experimental import pallas as pl
from jax.experimental.pallas import tpu as pltpu
from jax.sharding import PartitionSpec as P

J = 64
K = 128
GROUP = 4


def legendre_constants(degrees, columns):
    q = np.abs(np.arange(columns) - degrees).astype(np.float64)
    log_norm = np.array(
        [
            0.5
            * (
                math.log((2 * v + 1) / (4 * math.pi))
                + math.lgamma(2 * v + 1)
                - v * math.log(4.0)
                - 2 * math.lgamma(v + 1)
            )
            for v in q
        ]
    )
    l = np.arange(degrees, dtype=np.float64)[:, None]
    numer = np.maximum(4 * l * l - 1, 1.0)
    denom = np.maximum(l * l - q[None] ** 2, 1.0)
    factor = np.sqrt(numer / denom)
    before = np.ones_like(factor)
    before[1:] = 1.0 / factor[:-1]
    return (
        log_norm.astype(np.float32)[None],
        q.astype(np.float32)[None],
        factor.astype(np.float32)[:, None, :],
        before.astype(np.float32)[:, None, :],
    )


def wave_matrix(degrees, columns, azimuths):
    turns = ((np.arange(columns)[:, None] - degrees) * np.arange(azimuths)[None, :]) % azimuths
    angle = 2.0 * np.pi * turns / azimuths
    cosine, sine = np.cos(angle), np.sin(angle)
    left = np.concatenate([cosine, -sine], axis=0)
    right = np.concatenate([-sine, -cosine], axis=0)
    return np.concatenate([left, right], axis=1).astype(np.float32)


def phase_tables(polar, azimuths):
    azimuth = 2.0 * jnp.pi * jnp.arange(azimuths).astype(jnp.float32) / azimuths
    octants = jnp.arange(8, dtype=jnp.int32)
    dir_x = jnp.sin(polar)[:, None] * jnp.cos(azimuth)[None, :]
    dir_y = jnp.sin(polar)[:, None] * jnp.sin(azimuth)[None, :]
    dir_z = jnp.cos(polar)[:, None] * jnp.ones_like(azimuth)[None, :]
    sign_x = (2 * (octants & 1) - 1).astype(jnp.float32)[:, None, None]
    sign_y = (2 * (octants >> 1 & 1) - 1).astype(jnp.float32)[:, None, None]
    sign_z = (2 * (octants >> 2 & 1) - 1).astype(jnp.float32)[:, None, None]
    phase = 5.5 * (sign_x * dir_x[None] + sign_y * dir_y[None] + sign_z * dir_z[None])
    return jnp.repeat(jnp.cos(phase), 2, axis=1), jnp.repeat(jnp.sin(phase), 2, axis=1)


def fill_table(tab, diag_ref, cos_ref, order_ref, factor_ref, before_ref):
    degrees = tab.shape[0]
    diag = diag_ref[...]
    cosines = cos_ref[...]
    order = jnp.broadcast_to(order_ref[...], diag.shape)
    next_value = jnp.sqrt(2.0 * order + 3.0) * cosines * diag

    def advance(degree, state):
        previous, before = state
        level = lax.convert_element_type(degree, jnp.float32)
        recur = factor_ref[degree] * (cosines * previous - before * before_ref[degree])
        value = jnp.where(level == order + 1.0, next_value, recur)
        value = jnp.where(level == order, diag, value)
        value = jnp.where(level < order, 0.0, value)
        tab[degree] = value
        return value, previous

    zeros = diag - diag
    lax.fori_loop(0, degrees, advance, (zeros, zeros))


def transform(source, child, *refs):
    cycles = refs[:GROUP]
    matrix, phase_cos, phase_sin, out, upper, lower = refs[GROUP:]
    step = pl.program_id(0)
    _, lines, width, _ = cycles[0].shape
    cases = lines // 2
    rows = 2 * width
    for box in range(GROUP):
        for case in range(cases):
            base = (box * cases + case) * rows
            real, imag = cycles[box][0, 2 * case], cycles[box][0, 2 * case + 1]
            upper[pl.ds(base, width, 2), :] = real
            upper[pl.ds(base + 1, width, 2), :] = imag
            lower[pl.ds(base, width, 2), :] = imag
            lower[pl.ds(base + 1, width, 2), :] = -real
    both = jnp.concatenate([upper[...], lower[...]], axis=1)
    spread = jnp.dot(both, matrix[...], precision=lax.Precision.HIGHEST, preferred_element_type=jnp.float32)
    for box in range(GROUP):
        for place in range(8):
            octant = child[(step * GROUP + box) * 8 + place]
            turn_cos = phase_cos[octant]
            turn_sin = phase_sin[octant]
            for case in range(cases):
                base = (box * cases + case) * rows
                wave = spread[base : base + rows, :K]
                quarter = spread[base : base + rows, K:]
                out[box, case, place] = wave * turn_cos + quarter * turn_sin


def own_polar(parts, blk_index):
    width = J // parts
    polar_all = jnp.pi * (jnp.arange(J).astype(jnp.float32) + 0.5) / J
    return lax.dynamic_slice_in_dim(polar_all, blk_index * width, width, 0)


def make_children(cycles, source, child_list, parts, lines, blk_index):
    boxes, _, width, columns = cycles.shape
    cases = lines // 2
    phase_cos, phase_sin = phase_tables(own_polar(parts, blk_index), K)
    matrix = jnp.asarray(wave_matrix(columns // 2, columns, K))

    def pick(offset):
        return pl.BlockSpec(
            (1, lines, width, columns),
            lambda i, source, child: (source[i * GROUP + offset], 0, 0, 0),
        )

    whole = pl.BlockSpec(memory_space=pltpu.VMEM)
    rows = GROUP * cases * 2 * width
    out = pl.pallas_call(
        transform,
        grid_spec=pltpu.PrefetchScalarGridSpec(
            num_scalar_prefetch=2,
            grid=(boxes // GROUP,),
            in_specs=[pick(n) for n in range(GROUP)] + [whole] * 3,
            out_specs=pl.BlockSpec(
                (GROUP, cases, 8, 2 * width, K), lambda i, source, child: (i, 0, 0, 0, 0)
            ),
            scratch_shapes=[
                pltpu.VMEM((rows, columns), jnp.float32),
                pltpu.VMEM((rows, columns), jnp.float32),
            ],
        ),
        out_shape=jax.ShapeDtypeStruct((boxes, cases, 8, 2 * width, K), jnp.float32),
        compiler_params=pltpu.CompilerParams(vmem_limit_bytes=40 * 1024 * 1024),
        name="transform",
    )(source, child_list.reshape(-1), *([cycles] * GROUP), matrix, phase_cos, phase_sin)
    return out.reshape(boxes, cases, 8, width, 2, K)


def swapped(index, step, size):
    total = 0
    bit = 1
    while bit < size:
        total = total + ((index // bit + step // bit) % 2) * bit
        bit *= 2
    return total


def exchange(
    sub_count,
    chips,
    blocks,
    slots,
    diag,
    cosines,
    orders,
    factor,
    before,
    cycles,
    placed,
    gathered,
    tab,
    send_far,
    recv_far,
    send_near,
    recv_near,
    send_pair,
    recv_pair,
    send_slot,
    recv_slot,
    local,
):
    per_peer = blocks.shape[1]
    steps = sub_count * per_peer
    sub = lax.axis_index("sub")
    blk = lax.axis_index("blk")
    chip = blk // 2
    core = blk % 2
    sibling = chip * 2 + (1 - core)

    def remote(source, target, send, recv, device):
        return pltpu.make_async_remote_copy(
            src_ref=source,
            dst_ref=target,
            send_sem=send,
            recv_sem=recv,
            device_id=device,
            device_id_type=pl.DeviceIdType.MESH,
        )

    def far(step, box):
        peer = swapped(sub, step, sub_count)
        return remote(
            blocks.at[peer, box],
            gathered.at[blk, sub, box],
            send_far.at[step, box],
            recv_far.at[step, box],
            (peer, blk),
        )

    def slot_copy(step):
        peer = swapped(sub, step, sub_count)
        return remote(slots.at[peer], placed.at[sub], send_slot.at[step], recv_slot.at[step], (peer, blk))

    def held(hop):
        return ((chip + chips - hop) % chips) * 2 + core

    def near(hop, step, box, own):
        source = swapped(sub, step, sub_count)
        origin = blocks.at[sub, box] if own else gathered.at[blk, source, box]
        return remote(
            origin,
            gathered.at[blk, source, box],
            send_near.at[hop - 1, step, box],
            recv_near.at[hop - 1, step, box],
            (sub, ((chip + hop) % chips) * 2 + core),
        )

    def pair(hop, step, box, own=False):
        source = swapped(sub, step, sub_count)
        part = held(hop)
        origin = blocks.at[sub, box] if own else gathered.at[part, source, box]
        return remote(
            origin,
            gathered.at[part, source, box],
            send_pair.at[hop, step, box],
            recv_pair.at[hop, step, box],
            (sub, sibling),
        )

    barrier = pltpu.get_barrier_semaphore()

    def greet(device):
        pl.semaphore_signal(barrier, inc=1, device_id=device, device_id_type=pl.DeviceIdType.MESH)

    for step in range(1, sub_count):
        greet((swapped(sub, step, sub_count), blk))
    for hop in range(1, chips):
        greet((sub, ((chip + hop) % chips) * 2 + core))
    greet((sub, sibling))
    pl.semaphore_wait(barrier, sub_count - 1 + chips)

    order = list(range(sub_count // 2, sub_count)) + list(range(2, sub_count // 2))
    everyone = [1] + order
    for step in everyone:
        slot_copy(step).start()

    @pl.loop(0, per_peer)
    def _(box):
        far(1, box).start()

    @pl.loop(0, per_peer)
    def _(box):
        for step in order:
            far(step, box).start()

    keep_slot = pltpu.make_async_copy(slots.at[sub], placed.at[sub], local.at[0])
    keep_slot.start()
    keep_blocks = pltpu.make_async_copy(blocks.at[sub], gathered.at[blk, sub], local.at[1])
    keep_blocks.start()
    fill_table(tab, diag, cosines, orders, factor, before)

    parts, _, _, rows, columns = gathered.shape
    degrees, width, _ = tab.shape
    depth = degrees // parts
    lines = rows // depth

    def finish(step, box):
        source = swapped(sub, step, sub_count)
        for hop in range(chips):
            pair(hop, step, box, step == 0 and hop == 0).wait_recv()

        def add(part, total):
            for inner in range(depth):
                value = gathered[part, source, box, pl.ds(inner, lines, depth), :]
                total = total + value[:, None, :] * tab[part * depth + inner][None]
            return total

        zeros = jnp.broadcast_to((tab[0] - tab[0])[None], (lines, width, columns))
        cycles[source, box] = lax.fori_loop(0, parts, add, zeros)

    def relay(step, box):
        for hop in range(1, chips):
            near(hop, step, box, False).wait_recv()
            pair(hop, step, box).start()

    def arrive(step, box):
        if step > 0:
            far(step, box).wait_recv()
        for hop in range(1, chips):
            near(hop, step, box, step == 0).start()
        pair(0, step, box, step == 0).start()

    @pl.loop(0, per_peer)
    def _(box):
        arrive(0, box)

    @pl.loop(0, per_peer)
    def _(box):
        arrive(1, box)
        relay(0, box)

    keep_blocks.wait()
    for step in order:
        arrive(step, 0)
    relay(1, 0)
    finish(0, 0)

    @pl.loop(1, per_peer)
    def _(box):
        for step in order:
            arrive(step, box)
            relay(step, box - 1)
        relay(1, box)
        finish(0, box)
        finish(1, box - 1)

        @pl.when(box > 1)
        def _():
            for step in order:
                finish(step, box - 2)

    for step in order:
        relay(step, per_peer - 1)
    finish(1, per_peer - 1)
    for back in (2, 1):
        for step in order:
            finish(step, per_peer - back)

    @pl.loop(0, per_peer)
    def _(box):
        for step in range(sub_count):
            if step > 0:
                far(step, box).wait_send()
            for hop in range(1, chips):
                near(hop, step, box, step == 0).wait_send()
            for hop in range(chips):
                pair(hop, step, box, step == 0 and hop == 0).wait_send()

    for step in everyone:
        slot_copy(step).wait()
    keep_slot.wait()


def exchange_all(outgoing, slots, parts, depth, blk_index):
    sub_count, per_peer, rows, columns = outgoing.shape
    chips = parts // 2
    degrees = parts * depth
    width = J // parts
    lines = rows // depth
    polar = own_polar(parts, blk_index)
    log_norm, order, factor, before = legendre_constants(degrees, columns)
    diag = jnp.exp(log_norm + order * jnp.log(jnp.sin(polar))[:, None])
    cosines = jnp.broadcast_to(jnp.cos(polar)[:, None], (width, columns))
    dma = pltpu.SemaphoreType.DMA
    anywhere = pl.BlockSpec(memory_space=pl.ANY)
    vmem = pl.BlockSpec(memory_space=pltpu.VMEM)
    hops = max(chips - 1, 1)
    return pl.pallas_call(
        functools.partial(exchange, sub_count, chips),
        out_shape=(
            jax.ShapeDtypeStruct((sub_count, per_peer, lines, width, columns), jnp.float32),
            jax.ShapeDtypeStruct(slots.shape, jnp.int32),
        ),
        in_specs=[anywhere] + [vmem] * 6,
        out_specs=(vmem, vmem),
        scratch_shapes=[
            pltpu.VMEM((parts, sub_count, per_peer, rows, columns), jnp.float32),
            pltpu.VMEM((degrees, width, columns), jnp.float32),
            dma((sub_count, per_peer)),
            dma((sub_count, per_peer)),
            dma((hops, sub_count, per_peer)),
            dma((hops, sub_count, per_peer)),
            dma((chips, sub_count, per_peer)),
            dma((chips, sub_count, per_peer)),
            dma((sub_count,)),
            dma((sub_count,)),
            dma((2,)),
        ],
        compiler_params=pltpu.CompilerParams(
            collective_id=0, has_side_effects=True, vmem_limit_bytes=40 * 1024 * 1024
        ),
        name="exchange",
    )(
        outgoing,
        slots,
        diag,
        cosines,
        jnp.asarray(order),
        jnp.asarray(factor),
        jnp.asarray(before),
    )


def body(coefficients, owner_slot, child_list):
    box_count, cases, _, depth, columns = coefficients.shape
    sub_count = lax.axis_size("sub")
    parts = lax.axis_size("blk")
    per_peer = box_count // sub_count
    targets = owner_slot // box_count
    positions = owner_slot % box_count
    send_order = jnp.argsort(targets, stable=True)
    flat = coefficients.reshape(box_count, cases * 2 * depth, columns)
    outgoing = flat[send_order].reshape(sub_count, per_peer, cases * 2 * depth, columns)
    slots = positions[send_order].reshape(sub_count, 1, per_peer)
    slots = jnp.pad(slots, ((0, 0), (0, 0), (0, 128 - per_peer)))
    blk_index = lax.axis_index("blk")
    cycles, placed = exchange_all(outgoing, slots, parts, depth, blk_index)
    source = jnp.argsort(placed[:, 0, :per_peer].reshape(-1)).astype(jnp.int32)
    cycles = cycles.reshape((box_count,) + cycles.shape[2:])
    return make_children(cycles, source, child_list, parts, 2 * cases, blk_index)


def solution(mesh):
    placed = (P("sub", None, None, "blk", None), P("sub"), P("sub", None))
    return jax.shard_map(
        body,
        mesh=mesh,
        in_specs=placed,
        out_specs=P("sub", None, None, "blk", None, None),
        check_vma=False,
    )
```

```python
import functools
import math

import jax
import jax.numpy as jnp
import numpy as np
from jax import lax
from jax.experimental import pallas as pl
from jax.experimental.pallas import tpu as pltpu
from jax.sharding import PartitionSpec as P

J = 64
K = 128
GROUP = 4


def legendre_constants(degrees, columns):
    q = np.abs(np.arange(columns) - degrees).astype(np.float64)
    log_norm = np.array(
        [
            0.5
            * (
                math.log((2 * v + 1) / (4 * math.pi))
                + math.lgamma(2 * v + 1)
                - v * math.log(4.0)
                - 2 * math.lgamma(v + 1)
            )
            for v in q
        ]
    )
    l = np.arange(degrees, dtype=np.float64)[:, None]
    numer = np.maximum(4 * l * l - 1, 1.0)
    denom = np.maximum(l * l - q[None] ** 2, 1.0)
    factor = np.sqrt(numer / denom)
    before = np.ones_like(factor)
    before[1:] = 1.0 / factor[:-1]
    return (
        log_norm.astype(np.float32)[None],
        q.astype(np.float32)[None],
        factor.astype(np.float32)[:, None, :],
        before.astype(np.float32)[:, None, :],
    )


def wave_matrix(degrees, columns, azimuths):
    turns = ((np.arange(columns)[:, None] - degrees) * np.arange(azimuths)[None, :]) % azimuths
    angle = 2.0 * np.pi * turns / azimuths
    cosine, sine = np.cos(angle), np.sin(angle)
    left = np.concatenate([cosine, -sine], axis=0)
    right = np.concatenate([-sine, -cosine], axis=0)
    return np.concatenate([left, right], axis=1).astype(np.float32)


def phase_tables(polar, azimuths):
    azimuth = 2.0 * jnp.pi * jnp.arange(azimuths).astype(jnp.float32) / azimuths
    octants = jnp.arange(8, dtype=jnp.int32)
    dir_x = jnp.sin(polar)[:, None] * jnp.cos(azimuth)[None, :]
    dir_y = jnp.sin(polar)[:, None] * jnp.sin(azimuth)[None, :]
    dir_z = jnp.cos(polar)[:, None] * jnp.ones_like(azimuth)[None, :]
    sign_x = (2 * (octants & 1) - 1).astype(jnp.float32)[:, None, None]
    sign_y = (2 * (octants >> 1 & 1) - 1).astype(jnp.float32)[:, None, None]
    sign_z = (2 * (octants >> 2 & 1) - 1).astype(jnp.float32)[:, None, None]
    phase = 5.5 * (sign_x * dir_x[None] + sign_y * dir_y[None] + sign_z * dir_z[None])
    return jnp.repeat(jnp.cos(phase), 2, axis=1), jnp.repeat(jnp.sin(phase), 2, axis=1)


def fill_table(tab, diag_ref, cos_ref, order_ref, factor_ref, before_ref):
    degrees = tab.shape[0]
    diag = diag_ref[...]
    cosines = cos_ref[...]
    order = jnp.broadcast_to(order_ref[...], diag.shape)
    next_value = jnp.sqrt(2.0 * order + 3.0) * cosines * diag

    def advance(degree, state):
        previous, before = state
        level = lax.convert_element_type(degree, jnp.float32)
        recur = factor_ref[degree] * (cosines * previous - before * before_ref[degree])
        value = jnp.where(level == order + 1.0, next_value, recur)
        value = jnp.where(level == order, diag, value)
        value = jnp.where(level < order, 0.0, value)
        tab[degree] = value
        return value, previous

    zeros = diag - diag
    lax.fori_loop(0, degrees, advance, (zeros, zeros))


def transform(source, child, *refs):
    cycles = refs[:GROUP]
    matrix, phase_cos, phase_sin, out, upper, lower = refs[GROUP:]
    step = pl.program_id(0)
    _, lines, width, _ = cycles[0].shape
    cases = lines // 2
    rows = 2 * width
    for box in range(GROUP):
        for case in range(cases):
            base = (box * cases + case) * rows
            real, imag = cycles[box][0, 2 * case], cycles[box][0, 2 * case + 1]
            upper[pl.ds(base, width, 2), :] = real
            upper[pl.ds(base + 1, width, 2), :] = imag
            lower[pl.ds(base, width, 2), :] = imag
            lower[pl.ds(base + 1, width, 2), :] = -real
    both = jnp.concatenate([upper[...], lower[...]], axis=1)
    spread = jnp.dot(both, matrix[...], precision=lax.Precision.HIGHEST, preferred_element_type=jnp.float32)
    for box in range(GROUP):
        for place in range(8):
            octant = child[(step * GROUP + box) * 8 + place]
            turn_cos = phase_cos[octant]
            turn_sin = phase_sin[octant]
            for case in range(cases):
                base = (box * cases + case) * rows
                wave = spread[base : base + rows, :K]
                quarter = spread[base : base + rows, K:]
                out[box, case, place] = wave * turn_cos + quarter * turn_sin


def own_polar(parts, blk_index):
    width = J // parts
    polar_all = jnp.pi * (jnp.arange(J).astype(jnp.float32) + 0.5) / J
    return lax.dynamic_slice_in_dim(polar_all, blk_index * width, width, 0)


def make_children(cycles, source, child_list, parts, lines, blk_index):
    boxes, _, width, columns = cycles.shape
    cases = lines // 2
    phase_cos, phase_sin = phase_tables(own_polar(parts, blk_index), K)
    matrix = jnp.asarray(wave_matrix(columns // 2, columns, K))

    def pick(offset):
        return pl.BlockSpec(
            (1, lines, width, columns),
            lambda i, source, child: (source[i * GROUP + offset], 0, 0, 0),
        )

    whole = pl.BlockSpec(memory_space=pltpu.VMEM)
    rows = GROUP * cases * 2 * width
    out = pl.pallas_call(
        transform,
        grid_spec=pltpu.PrefetchScalarGridSpec(
            num_scalar_prefetch=2,
            grid=(boxes // GROUP,),
            in_specs=[pick(n) for n in range(GROUP)] + [whole] * 3,
            out_specs=pl.BlockSpec(
                (GROUP, cases, 8, 2 * width, K), lambda i, source, child: (i, 0, 0, 0, 0)
            ),
            scratch_shapes=[
                pltpu.VMEM((rows, columns), jnp.float32),
                pltpu.VMEM((rows, columns), jnp.float32),
            ],
        ),
        out_shape=jax.ShapeDtypeStruct((boxes, cases, 8, 2 * width, K), jnp.float32),
        compiler_params=pltpu.CompilerParams(vmem_limit_bytes=40 * 1024 * 1024),
        name="transform",
    )(source, child_list.reshape(-1), *([cycles] * GROUP), matrix, phase_cos, phase_sin)
    return out.reshape(boxes, cases, 8, width, 2, K)


def swapped(index, step, size):
    total = 0
    bit = 1
    while bit < size:
        total = total + ((index // bit + step // bit) % 2) * bit
        bit *= 2
    return total


def exchange(
    sub_count,
    chips,
    blocks,
    slots,
    diag,
    cosines,
    orders,
    factor,
    before,
    cycles,
    placed,
    gathered,
    tab,
    send_far,
    recv_far,
    send_near,
    recv_near,
    send_pair,
    recv_pair,
    send_slot,
    recv_slot,
    local,
):
    per_peer = blocks.shape[1]
    steps = sub_count * per_peer
    sub = lax.axis_index("sub")
    blk = lax.axis_index("blk")
    chip = blk // 2
    core = blk % 2
    sibling = chip * 2 + (1 - core)

    def remote(source, target, send, recv, device):
        return pltpu.make_async_remote_copy(
            src_ref=source,
            dst_ref=target,
            send_sem=send,
            recv_sem=recv,
            device_id=device,
            device_id_type=pl.DeviceIdType.MESH,
        )

    def far(step, box):
        peer = swapped(sub, step, sub_count)
        return remote(
            blocks.at[peer, box],
            gathered.at[blk, sub, box],
            send_far.at[step, box],
            recv_far.at[step, box],
            (peer, blk),
        )

    def slot_copy(step):
        peer = swapped(sub, step, sub_count)
        return remote(slots.at[peer], placed.at[sub], send_slot.at[step], recv_slot.at[step], (peer, blk))

    def held(hop):
        return ((chip + chips - hop) % chips) * 2 + core

    def near(hop, step, box, own):
        source = swapped(sub, step, sub_count)
        origin = blocks.at[sub, box] if own else gathered.at[blk, source, box]
        return remote(
            origin,
            gathered.at[blk, source, box],
            send_near.at[hop - 1, step, box],
            recv_near.at[hop - 1, step, box],
            (sub, ((chip + hop) % chips) * 2 + core),
        )

    def pair(hop, step, box, own=False):
        source = swapped(sub, step, sub_count)
        part = held(hop)
        origin = blocks.at[sub, box] if own else gathered.at[part, source, box]
        return remote(
            origin,
            gathered.at[part, source, box],
            send_pair.at[hop, step, box],
            recv_pair.at[hop, step, box],
            (sub, sibling),
        )

    barrier = pltpu.get_barrier_semaphore()

    def greet(device):
        pl.semaphore_signal(barrier, inc=1, device_id=device, device_id_type=pl.DeviceIdType.MESH)

    for step in range(1, sub_count):
        greet((swapped(sub, step, sub_count), blk))
    for hop in range(1, chips):
        greet((sub, ((chip + hop) % chips) * 2 + core))
    greet((sub, sibling))
    pl.semaphore_wait(barrier, sub_count - 1 + chips)

    def relay(step, box):
        for hop in range(1, chips):
            near(hop, step, box, False).wait_recv()
            pair(hop, step, box).start()

    def arrive(step, box):
        if step > 0:
            far(step, box).wait_recv()
        for hop in range(1, chips):
            near(hop, step, box, step == 0).start()
        pair(0, step, box, step == 0).start()

    order = list(range(sub_count // 2, sub_count)) + list(range(2, sub_count // 2))
    everyone = [1] + order
    for step in everyone:
        slot_copy(step).start()

    @pl.loop(0, per_peer)
    def _(box):
        arrive(0, box)
        far(1, box).start()

        @pl.when(box < 2)
        def _():
            for step in order:
                far(step, box).start()

    keep_slot = pltpu.make_async_copy(slots.at[sub], placed.at[sub], local.at[0])
    keep_slot.start()
    keep_blocks = pltpu.make_async_copy(blocks.at[sub], gathered.at[blk, sub], local.at[1])
    keep_blocks.start()
    fill_table(tab, diag, cosines, orders, factor, before)

    parts, _, _, rows, columns = gathered.shape
    degrees, width, _ = tab.shape
    depth = degrees // parts
    lines = rows // depth

    def finish(step, box):
        source = swapped(sub, step, sub_count)
        for hop in range(chips):
            pair(hop, step, box, step == 0 and hop == 0).wait_recv()

        def add(part, total):
            for inner in range(depth):
                value = gathered[part, source, box, pl.ds(inner, lines, depth), :]
                total = total + value[:, None, :] * tab[part * depth + inner][None]
            return total

        zeros = jnp.broadcast_to((tab[0] - tab[0])[None], (lines, width, columns))
        cycles[source, box] = lax.fori_loop(0, parts, add, zeros)

    @pl.loop(0, per_peer)
    def _(box):
        arrive(1, box)
        relay(0, box)

    keep_blocks.wait()
    for step in order:
        arrive(step, 0)
    relay(1, 0)
    finish(0, 0)

    @pl.loop(1, per_peer)
    def _(box):
        @pl.when(box + 1 < per_peer)
        def _():
            for step in order:
                far(step, box + 1).start()

        for step in order:
            arrive(step, box)
            relay(step, box - 1)
        relay(1, box)
        finish(0, box)
        finish(1, box - 1)

        @pl.when(box > 1)
        def _():
            for step in order:
                finish(step, box - 2)

    for step in order:
        relay(step, per_peer - 1)
    finish(1, per_peer - 1)
    for back in (2, 1):
        for step in order:
            finish(step, per_peer - back)

    @pl.loop(0, per_peer)
    def _(box):
        for step in range(sub_count):
            if step > 0:
                far(step, box).wait_send()
            for hop in range(1, chips):
                near(hop, step, box, step == 0).wait_send()
            for hop in range(chips):
                pair(hop, step, box, step == 0 and hop == 0).wait_send()

    for step in everyone:
        slot_copy(step).wait()
    keep_slot.wait()


def exchange_all(outgoing, slots, parts, depth, blk_index):
    sub_count, per_peer, rows, columns = outgoing.shape
    chips = parts // 2
    degrees = parts * depth
    width = J // parts
    lines = rows // depth
    polar = own_polar(parts, blk_index)
    log_norm, order, factor, before = legendre_constants(degrees, columns)
    diag = jnp.exp(log_norm + order * jnp.log(jnp.sin(polar))[:, None])
    cosines = jnp.broadcast_to(jnp.cos(polar)[:, None], (width, columns))
    dma = pltpu.SemaphoreType.DMA
    anywhere = pl.BlockSpec(memory_space=pl.ANY)
    vmem = pl.BlockSpec(memory_space=pltpu.VMEM)
    hops = max(chips - 1, 1)
    return pl.pallas_call(
        functools.partial(exchange, sub_count, chips),
        out_shape=(
            jax.ShapeDtypeStruct((sub_count, per_peer, lines, width, columns), jnp.float32),
            jax.ShapeDtypeStruct(slots.shape, jnp.int32),
        ),
        in_specs=[anywhere] + [vmem] * 6,
        out_specs=(vmem, vmem),
        scratch_shapes=[
            pltpu.VMEM((parts, sub_count, per_peer, rows, columns), jnp.float32),
            pltpu.VMEM((degrees, width, columns), jnp.float32),
            dma((sub_count, per_peer)),
            dma((sub_count, per_peer)),
            dma((hops, sub_count, per_peer)),
            dma((hops, sub_count, per_peer)),
            dma((chips, sub_count, per_peer)),
            dma((chips, sub_count, per_peer)),
            dma((sub_count,)),
            dma((sub_count,)),
            dma((2,)),
        ],
        compiler_params=pltpu.CompilerParams(
            collective_id=0, has_side_effects=True, vmem_limit_bytes=40 * 1024 * 1024
        ),
        name="exchange",
    )(
        outgoing,
        slots,
        diag,
        cosines,
        jnp.asarray(order),
        jnp.asarray(factor),
        jnp.asarray(before),
    )


def body(coefficients, owner_slot, child_list):
    box_count, cases, _, depth, columns = coefficients.shape
    sub_count = lax.axis_size("sub")
    parts = lax.axis_size("blk")
    per_peer = box_count // sub_count
    targets = owner_slot // box_count
    positions = owner_slot % box_count
    send_order = jnp.argsort(targets, stable=True)
    flat = coefficients.reshape(box_count, cases * 2 * depth, columns)
    outgoing = flat[send_order].reshape(sub_count, per_peer, cases * 2 * depth, columns)
    slots = positions[send_order].reshape(sub_count, 1, per_peer)
    slots = jnp.pad(slots, ((0, 0), (0, 0), (0, 128 - per_peer)))
    blk_index = lax.axis_index("blk")
    cycles, placed = exchange_all(outgoing, slots, parts, depth, blk_index)
    source = jnp.argsort(placed[:, 0, :per_peer].reshape(-1)).astype(jnp.int32)
    cycles = cycles.reshape((box_count,) + cycles.shape[2:])
    return make_children(cycles, source, child_list, parts, 2 * cases, blk_index)


def solution(mesh):
    placed = (P("sub", None, None, "blk", None), P("sub"), P("sub", None))
    return jax.shard_map(
        body,
        mesh=mesh,
        in_specs=placed,
        out_specs=P("sub", None, None, "blk", None, None),
        check_vma=False,
    )
```
